512 devices in a mesh: pair: 128 (over z, x, core), red: 4 (over y).
Axes of the slice: x: 4, y: 4, z: 16, core: 2. Of those that a mesh axis runs over, the one named last changes fastest.
Arguments:
- amplitudes: bfloat16 [256, 128, 1024], P('pair', None, 'red'), may hold values from -6 to 6
- ladder_ints: bfloat16 [128, 1024, 1024], P('pair', 'red'), may hold values from -0.25 to 0.25
- live_count: int32 [128], replicated, may hold values from 128 to 1024, as said below
Outputs:
- residual: bfloat16 [256, 128, 1024], P('pair', None, 'red')
The draws below stay inside these ranges and needn't reach their ends.
Inputs may be any that keep to these rules, and one draw needn't show every extreme that they name: Only contracted pairs c < live_count[s] of slab s take part; in every draw some slab has all 1024 pairs live.
All inputs are finite; a program needn't handle non-finite values.
Results may differ from the reference program's by a relative error of at most 0.012.
Values may be sent and summed in bfloat16 or wider, within the bound.
A program may use at most 128 MiB of HBM per device.

```python
import jax
import jax.numpy as jnp
from jax import lax

CD_DEV = 256
OP = 256
NSLAB = 128
VPS = 1024
AB = 1024
N_RED = 4


def draw_live_count(key, part):
    first, second = jax.random.split(key)
    counts = jax.random.randint(first, (NSLAB,), VPS // 8, VPS + 1)
    chosen = jax.random.randint(second, (), 0, NSLAB)
    return jnp.where(jnp.arange(NSLAB) == chosen, VPS, counts).astype(jnp.int32)


def strengthened(result, rng, source, target, shards_of, factor):
    def block_of(dim):
        return (jnp.arange(result.shape[dim]) // (result.shape[dim] // shards_of)).reshape((-1,) + (1,) * (result.ndim - 1 - dim))

    first = jax.random.permutation(rng, shards_of)[block_of(target)]
    other_side = (block_of(target) + shards_of // 2) % shards_of
    return jnp.where((block_of(source) == first) | (block_of(source) == other_side), factor * result, result)


def block_scale(own_key, shape, pieces, least, high):
    level = 1.0
    for axis_at, blocks in pieces:
        steps = jax.random.uniform(jax.random.fold_in(jax.random.fold_in(own_key, 6), axis_at), (blocks,), jnp.float32, least / len(pieces), high / len(pieces))
        level = level * jnp.repeat(jnp.exp(steps), shape[axis_at] // blocks).reshape((-1,) + (1,) * (len(shape) - 1 - axis_at))
    return level


def scatter_about(stream_key, shape, deviation, reach, cuts=(), kind=jnp.bfloat16):
    array = deviation * jax.random.normal(stream_key, shape, jnp.float32)
    if cuts:
        array = array * block_scale(stream_key, shape, cuts, -0.22, 0.18)
    return jnp.clip(array, -reach, reach).astype(kind)


def heavy_noise(own_key, shape, spread, limit, pieces, heavy, kind=jnp.bfloat16):
    result = spread * jax.random.normal(own_key, shape, jnp.float32)
    if pieces:
        result = result * block_scale(own_key, shape, pieces, -0.22, 0.18)
    return jnp.clip(strengthened(result, jax.random.fold_in(own_key, 3), *heavy), -limit, limit).astype(kind)


def setup_inputs(seed: int = 0) -> dict:
    key_list = jax.random.split(jax.random.key(seed), 4)
    return {
        "amplitudes": scatter_about(key_list[0], (OP, NSLAB, VPS), 1.0, 6.0, ((0, 128), (2, 4))),
        "ladder_ints": heavy_noise(key_list[1], (NSLAB, VPS, AB), VPS ** -0.5, 0.25, ((0, 128), (1, 4)), (1, 2, 4, 2.0)),
        "live_count": draw_live_count(jax.random.fold_in(key_list[3], 71), 0),
    }


def reference(amplitudes, ladder_ints, live_count):
    position = jnp.arange(VPS, dtype=jnp.int32)

    def one_slab(items):
        block, integrals, count = items
        masked = jnp.where(position[None, :] < count, block, jnp.zeros_like(block))
        left = masked.astype(jnp.float32).reshape(OP, N_RED, CD_DEV)
        right = integrals.astype(jnp.float32).reshape(N_RED, CD_DEV, AB)
        shares = jnp.einsum("ork,rka->roa", left, right, precision=lax.Precision.HIGHEST)
        rounded = lax.optimization_barrier(shares.astype(jnp.bfloat16))
        return jnp.sum(rounded.astype(jnp.float32), axis=0)

    ladder = lax.map(one_slab, (jnp.moveaxis(amplitudes, 1, 0), ladder_ints, live_count))
    return jnp.moveaxis(ladder, 0, 1).astype(jnp.bfloat16)
```

```python
import functools

import jax
import jax.numpy as jnp
from jax import lax
from jax.experimental import pallas as pl
from jax.experimental.pallas import tpu as pltpu
from jax.sharding import PartitionSpec as P

MESH = pl.DeviceIdType.MESH
NZ = 16
NX = 8
NR = 4
PLANES = 2
CHUNKS = NZ // PLANES
FAR = [8] + [d for i in range(7, 0, -1) for d in (i, 16 - i)]


def kernel(amp_ref, w_ref, live_ref, out_ref, amp, w, live, xs, ra, rb, pb, rr, ob,
           lsem, asem, bsem, rsem, osem, asend, bsend, rsend, osend, ready):
    me = lax.axis_index("pair")
    r = lax.axis_index("red")
    z = me // NX
    xc = lax.rem(me, NX)

    barrier = pltpu.get_barrier_semaphore()
    for k in range(1, NZ):
        pl.semaphore_signal(barrier, inc=1, device_id=(lax.rem(z + k, NZ) * NX + xc, r), device_id_type=MESH)
    for k in range(1, NX):
        pl.semaphore_signal(barrier, inc=1, device_id=(z * NX + lax.rem(xc + k, NX), r), device_id_type=MESH)
    for k in range(1, NR):
        pl.semaphore_signal(barrier, inc=1, device_id=(me, lax.rem(r + k, NR)), device_id_type=MESH)

    loads = [pltpu.make_async_copy(amp_ref, amp, lsem.at[0]),
             pltpu.make_async_copy(w_ref, w, lsem.at[1]),
             pltpu.make_async_copy(live_ref, live, lsem.at[2])]
    for copy in loads:
        copy.start()
    loads[0].wait()
    xs[...] = jnp.stack([amp[0], amp[1]], axis=1).reshape(NZ, NX, 2, 256)
    loads[1].wait()
    loads[2].wait()
    limit = live[me] - r * 256
    rows = lax.broadcasted_iota(jnp.int32, (256, 1024), 0)
    w[0] = jnp.where(rows < limit, w[0], jnp.zeros_like(w[0]))

    pl.semaphore_wait(barrier, NZ + NX + NR - 3)
    for k in FAR:
        zz = lax.rem(z + k, NZ)
        pltpu.make_async_remote_copy(xs.at[zz], ra.at[z], asend, asem.at[z // PLANES],
                                     device_id=(zz * NX + xc, r), device_id_type=MESH).start()
    pltpu.make_async_copy(xs.at[z], ra.at[z], asem.at[z // PLANES]).start()
    for k in range(1, NX):
        pl.semaphore_signal(ready, inc=1, device_id=(z * NX + lax.rem(xc + k, NX), r), device_id_type=MESH)

    def forward(c):
        span = pl.ds(c * PLANES, PLANES)
        pltpu.make_async_copy(ra.at[span], ra.at[span], asem.at[c]).wait()
        for k in range(1, NX):
            q = lax.rem(xc + k, NX)
            pltpu.make_async_remote_copy(ra.at[span, q], rb.at[span, xc], bsend, bsem.at[c],
                                         device_id=(z * NX + q, r), device_id_type=MESH).start()
        pltpu.make_async_copy(ra.at[span, xc], rb.at[span, xc], bsem.at[c]).start()

    def multiply(c):
        span = pl.ds(c * PLANES, PLANES)
        pltpu.make_async_copy(rb.at[span], rb.at[span], bsem.at[c]).wait()
        rows = rb[span].reshape(PLANES * NX * 2, 256)
        part = jnp.dot(rows, w[0], preferred_element_type=jnp.float32).astype(jnp.bfloat16)
        for j in range(NR):
            pb[c, j] = part[:, j * 256:(j + 1) * 256]
        for k in (2, 1, 3):
            rk = lax.rem(r + k, NR)
            pltpu.make_async_remote_copy(pb.at[c, rk], rr.at[c, k - 1], rsend, rsem.at[c],
                                         device_id=(me, rk), device_id_type=MESH).start()

    def reduce(c):
        pltpu.make_async_copy(rr.at[c], rr.at[c], rsem.at[c]).wait()
        total = pb[c, r].astype(jnp.float32)
        for k in range(NR - 1):
            total = total + rr[c, k].astype(jnp.float32)
        ob[pl.ds(c * PLANES * NX, PLANES * NX)] = total.astype(jnp.bfloat16).reshape(PLANES * NX, 2, 256)

        def send(i, carry):
            p = c * PLANES * NX + i

            @pl.when(p != me)
            def _():
                pltpu.make_async_remote_copy(ob.at[p], out_ref.at[me], osend, osem,
                                             device_id=(p, r), device_id_type=MESH).start()

            @pl.when(p == me)
            def _():
                pltpu.make_async_copy(ob.at[p], out_ref.at[me], osem).start()

            return carry

        lax.fori_loop(0, PLANES * NX, send, 0)

    for t in range(CHUNKS + 2):
        if t < CHUNKS:
            forward(t)
        if 0 <= t - 1 < CHUNKS:
            multiply(t - 1)
        if t == 2:
            pl.semaphore_wait(ready, NX - 1)
        if 0 <= t - 2 < CHUNKS:
            reduce(t - 2)

    pltpu.make_async_copy(out_ref, out_ref, osem).wait()
    pltpu.make_async_copy(xs.at[pl.ds(0, NZ - 1)], xs.at[pl.ds(0, NZ - 1)], asend).wait()
    pltpu.make_async_copy(rb.at[:, pl.ds(0, NX - 1)], rb.at[:, pl.ds(0, NX - 1)], bsend).wait()
    pltpu.make_async_copy(rr, rr, rsend).wait()
    pltpu.make_async_copy(ob.at[pl.ds(0, NZ * NX - 1)], ob.at[pl.ds(0, NZ * NX - 1)], osend).wait()


def body(amplitudes, ladder_ints, live_count):
    any_space = pl.BlockSpec(memory_space=pl.ANY)
    bf16 = jnp.bfloat16
    out = pl.pallas_call(
        kernel,
        out_shape=jax.ShapeDtypeStruct((NZ * NX, 2, 256), bf16),
        in_specs=[any_space] * 3,
        out_specs=any_space,
        scratch_shapes=[
            pltpu.VMEM((2, 128, 256), bf16),
            pltpu.VMEM((1, 256, 1024), bf16),
            pltpu.SMEM((128,), jnp.int32),
            pltpu.VMEM((NZ, NX, 2, 256), bf16),
            pltpu.VMEM((NZ, NX, 2, 256), bf16),
            pltpu.VMEM((NZ, NX, 2, 256), bf16),
            pltpu.VMEM((CHUNKS, NR, PLANES * NX * 2, 256), bf16),
            pltpu.VMEM((CHUNKS, NR - 1, PLANES * NX * 2, 256), bf16),
            pltpu.VMEM((NZ * NX, 2, 256), bf16),
            pltpu.SemaphoreType.DMA((3,)),
            pltpu.SemaphoreType.DMA((CHUNKS,)),
            pltpu.SemaphoreType.DMA((CHUNKS,)),
            pltpu.SemaphoreType.DMA((CHUNKS,)),
            pltpu.SemaphoreType.DMA,
            pltpu.SemaphoreType.DMA,
            pltpu.SemaphoreType.DMA,
            pltpu.SemaphoreType.DMA,
            pltpu.SemaphoreType.DMA,
            pltpu.SemaphoreType.REGULAR,
        ],
        compiler_params=pltpu.CompilerParams(collective_id=0, has_side_effects=True),
    )(amplitudes, ladder_ints, live_count)
    return jnp.transpose(out, (1, 0, 2))


def solution(mesh):
    in_specs = (P("pair", None, "red"), P("pair", "red", None), P())
    out_specs = P("pair", None, "red")
    return jax.shard_map(body, mesh=mesh, in_specs=in_specs, out_specs=out_specs, check_vma=False)
```

```python
import jax
import jax.numpy as jnp
from jax import lax
from jax.experimental import pallas as pl
from jax.experimental.pallas import tpu as pltpu
from jax.sharding import PartitionSpec as P

MESH = pl.DeviceIdType.MESH
NZ = 16
NX = 8
NR = 4
PLANES = 2
CHUNKS = NZ // PLANES
LAG = 5
PAIRS = PLANES * NX
FAR = [8] + [d for i in range(7, 0, -1) for d in (i, 16 - i)]


def kernel(amp_ref, w_ref, live_ref, out_ref, amp, w, live, xs, rb, pb, rr, ob,
           lsem, bsem, rsem, osem, bsend, rsend, osend):
    me = lax.axis_index("pair")
    r = lax.axis_index("red")
    z = me // NX
    xc = lax.rem(me, NX)

    partners = [lax.rem(z + dz, NZ) * NX + lax.rem(xc + k, NX)
                for dz in FAR + [0] for k in range(NX) if (dz, k) != (0, 0)]

    barrier = pltpu.get_barrier_semaphore()
    for p in partners:
        pl.semaphore_signal(barrier, inc=1, device_id=(p, r), device_id_type=MESH)
    for k in range(1, NR):
        pl.semaphore_signal(barrier, inc=1, device_id=(me, lax.rem(r + k, NR)), device_id_type=MESH)

    loads = [pltpu.make_async_copy(amp_ref, amp, lsem.at[0]),
             pltpu.make_async_copy(w_ref, w, lsem.at[1]),
             pltpu.make_async_copy(live_ref, live, lsem.at[2])]
    for copy in loads:
        copy.start()
    loads[0].wait()
    xs[...] = jnp.stack([amp[0], amp[1]], axis=1)
    loads[1].wait()
    loads[2].wait()
    limit = live[me] - r * 256
    rows = lax.broadcasted_iota(jnp.int32, (256, 1024), 0)
    w[0] = jnp.where(rows < limit, w[0], jnp.zeros_like(w[0]))

    pl.semaphore_wait(barrier, NZ * NX - 1 + NR - 1)
    for p in partners:
        pltpu.make_async_remote_copy(xs.at[p], rb.at[me], bsend, bsem.at[z // PLANES],
                                     device_id=(p, r), device_id_type=MESH).start()
    pltpu.make_async_copy(xs.at[me], rb.at[me], bsem.at[z // PLANES]).start()

    def multiply(c):
        span = pl.ds(c * PAIRS, PAIRS)
        pltpu.make_async_copy(rb.at[span], rb.at[span], bsem.at[c]).wait()
        rows = rb[span].reshape(PAIRS * 2, 256)
        part = jnp.dot(rows, w[0], preferred_element_type=jnp.float32).astype(jnp.bfloat16)
        for j in range(NR):
            pb[c, j] = part[:, j * 256:(j + 1) * 256]
        for k in (2, 1, 3):
            rk = lax.rem(r + k, NR)
            pltpu.make_async_remote_copy(pb.at[c, rk], rr.at[c, k - 1], rsend, rsem.at[c],
                                         device_id=(me, rk), device_id_type=MESH).start()

    def reduce(c):
        pltpu.make_async_copy(rr.at[c], rr.at[c], rsem.at[c]).wait()
        total = pb[c, r].astype(jnp.float32)
        for k in range(NR - 1):
            total = total + rr[c, k].astype(jnp.float32)
        ob[pl.ds(c * PAIRS, PAIRS)] = total.astype(jnp.bfloat16).reshape(PAIRS, 2, 256)

        def send(i, carry):
            p = c * PAIRS + i

            @pl.when(p != me)
            def _():
                pltpu.make_async_remote_copy(ob.at[p], out_ref.at[me], osend, osem,
                                             device_id=(p, r), device_id_type=MESH).start()

            @pl.when(p == me)
            def _():
                pltpu.make_async_copy(ob.at[p], out_ref.at[me], osem).start()

            return carry

        lax.fori_loop(0, PAIRS, send, 0)

    for t in range(CHUNKS + LAG):
        if t < CHUNKS:
            multiply(t)
        if t >= LAG:
            reduce(t - LAG)

    pltpu.make_async_copy(out_ref, out_ref, osem).wait()
    pltpu.make_async_copy(xs.at[pl.ds(0, NZ * NX - 1)], xs.at[pl.ds(0, NZ * NX - 1)], bsend).wait()
    pltpu.make_async_copy(rr, rr, rsend).wait()
    pltpu.make_async_copy(ob.at[pl.ds(0, NZ * NX - 1)], ob.at[pl.ds(0, NZ * NX - 1)], osend).wait()


def body(amplitudes, ladder_ints, live_count):
    any_space = pl.BlockSpec(memory_space=pl.ANY)
    bf16 = jnp.bfloat16
    out = pl.pallas_call(
        kernel,
        out_shape=jax.ShapeDtypeStruct((NZ * NX, 2, 256), bf16),
        in_specs=[any_space] * 3,
        out_specs=any_space,
        scratch_shapes=[
            pltpu.VMEM((2, 128, 256), bf16),
            pltpu.VMEM((1, 256, 1024), bf16),
            pltpu.SMEM((128,), jnp.int32),
            pltpu.VMEM((NZ * NX, 2, 256), bf16),
            pltpu.VMEM((NZ * NX, 2, 256), bf16),
            pltpu.VMEM((CHUNKS, NR, PAIRS * 2, 256), bf16),
            pltpu.VMEM((CHUNKS, NR - 1, PAIRS * 2, 256), bf16),
            pltpu.VMEM((NZ * NX, 2, 256), bf16),
            pltpu.SemaphoreType.DMA((3,)),
            pltpu.SemaphoreType.DMA((CHUNKS,)),
            pltpu.SemaphoreType.DMA((CHUNKS,)),
            pltpu.SemaphoreType.DMA,
            pltpu.SemaphoreType.DMA,
            pltpu.SemaphoreType.DMA,
            pltpu.SemaphoreType.DMA,
        ],
        compiler_params=pltpu.CompilerParams(collective_id=0, has_side_effects=True),
    )(amplitudes, ladder_ints, live_count)
    return jnp.transpose(out, (1, 0, 2))


def solution(mesh):
    in_specs = (P("pair", None, "red"), P("pair", "red", None), P())
    out_specs = P("pair", None, "red")
    return jax.shard_map(body, mesh=mesh, in_specs=in_specs, out_specs=out_specs, check_vma=False)
```

```python
import jax
import jax.numpy as jnp
from jax import lax
from jax.experimental import pallas as pl
from jax.experimental.pallas import tpu as pltpu
from jax.sharding import PartitionSpec as P

MESH = pl.DeviceIdType.MESH
NZ = 16
NX = 8
NR = 4
LAG = 4
SENDS = [8, 7, 9, 6, 10, 5, 11, 4, 12, 3, 13, 2, 14, 1, 15, 0]
MINE = SENDS.index(0) * NX
GROUPS = [(0,), (1,), (2,), (3,), (4, 5), (6, 7), (15, 14), (13, 12), (8, 9), (10, 11)]


def kernel(amp_ref, w_ref, live_ref, out_ref, amp, w, live, xs, rb, pb, rr, ob,
           lsem, bsem, rsem, osem, bsend, rsend, osend):
    me = lax.axis_index("pair")
    r = lax.axis_index("red")
    z = me // NX
    xc = lax.rem(me, NX)

    partners = []
    for dz in SENDS:
        for k in range(NX):
            if (dz, k) != (0, 0):
                partners.append(lax.rem(z + dz, NZ) * NX + lax.rem(xc + k, NX))

    loads = [pltpu.make_async_copy(amp_ref, amp, lsem.at[0]),
             pltpu.make_async_copy(w_ref, w, lsem.at[1]),
             pltpu.make_async_copy(live_ref, live, lsem.at[2])]
    for copy in loads:
        copy.start()

    barrier = pltpu.get_barrier_semaphore()
    for dz in range(1, NX):
        pl.semaphore_signal(barrier, inc=1, device_id=(z * NX + lax.rem(xc + dz, NX), r), device_id_type=MESH)
    for i in range(NZ - 1):
        zz = i + jnp.where(i >= z, 1, 0)
        for k in range(NX):
            pl.semaphore_signal(barrier, inc=1, device_id=(zz * NX + lax.rem(xc + k, NX), r), device_id_type=MESH)
    for k in range(1, NR):
        pl.semaphore_signal(barrier, inc=1, device_id=(me, lax.rem(r + k, NR)), device_id_type=MESH)

    loads[0].wait()
    xs[...] = jnp.stack([amp[0], amp[1]], axis=1)

    pl.semaphore_wait(barrier, NZ * NX - 1 + NR - 1)
    for p in partners:
        if p is partners[MINE]:
            pltpu.make_async_copy(xs.at[me], rb.at[me], bsem.at[z]).start()
        pltpu.make_async_remote_copy(xs.at[p], rb.at[me], bsend, bsem.at[z],
                                     device_id=(p, r), device_id_type=MESH).start()

    loads[1].wait()
    loads[2].wait()
    limit = live[me] - r * 256
    rows = lax.broadcasted_iota(jnp.int32, (256, 1024), 0)
    w[0] = jnp.where(rows < limit, w[0], jnp.zeros_like(w[0]))

    def multiply(g):
        parts = []
        for zz in GROUPS[g]:
            span = pl.ds(zz * NX, NX)
            pltpu.make_async_copy(rb.at[span], rb.at[span], bsem.at[zz]).wait()
            parts.append(rb[span].reshape(NX * 2, 256))
        rows = jnp.concatenate(parts, axis=0) if len(parts) > 1 else parts[0]
        height = pl.ds(0, rows.shape[0])
        part = jnp.dot(rows, w[0], preferred_element_type=jnp.float32).astype(jnp.bfloat16)
        for j in range(NR):
            pb[g, j, height] = part[:, j * 256:(j + 1) * 256]
        for k in (2, 1, 3):
            rk = lax.rem(r + k, NR)
            pltpu.make_async_remote_copy(pb.at[g, rk, height], rr.at[g, k - 1, height], rsend.at[g], rsem.at[g],
                                         device_id=(me, rk), device_id_type=MESH).start()

    def reduce(g):
        height = pl.ds(0, len(GROUPS[g]) * NX * 2)
        landed = rr.at[g, :, height]
        pltpu.make_async_copy(landed, landed, rsem.at[g]).wait()
        total = pb[g, r, height].astype(jnp.float32)
        for k in range(NR - 1):
            total = total + rr[g, k, height].astype(jnp.float32)
        total = total.astype(jnp.bfloat16)
        for i, zz in enumerate(GROUPS[g]):
            ob[pl.ds(zz * NX, NX)] = total[i * NX * 2:(i + 1) * NX * 2].reshape(NX, 2, 256)
        for zz in GROUPS[g]:
            @pl.when(zz == z)
            def _():
                pltpu.make_async_copy(ob.at[me], out_ref.at[me], osem).start()

            @pl.when(zz != z)
            def _():
                pltpu.make_async_remote_copy(ob.at[zz * NX + xc], out_ref.at[me], osend, osem,
                                             device_id=(zz * NX + xc, r), device_id_type=MESH).start()

            for k in range(1, NX):
                p = zz * NX + lax.rem(xc + k, NX)
                pltpu.make_async_remote_copy(ob.at[p], out_ref.at[me], osend, osem,
                                             device_id=(p, r), device_id_type=MESH).start()

    for t in range(len(GROUPS) + LAG):
        if t < len(GROUPS):
            multiply(t)
        if t >= LAG:
            reduce(t - LAG)

    pltpu.make_async_copy(out_ref, out_ref, osem).wait()
    pltpu.make_async_copy(xs.at[pl.ds(0, NZ * NX - 1)], xs.at[pl.ds(0, NZ * NX - 1)], bsend).wait()
    for g in range(len(GROUPS)):
        sent = rr.at[g, :, pl.ds(0, len(GROUPS[g]) * NX * 2)]
        pltpu.make_async_copy(sent, sent, rsend.at[g]).wait()
    pltpu.make_async_copy(ob.at[pl.ds(0, NZ * NX - 1)], ob.at[pl.ds(0, NZ * NX - 1)], osend).wait()


def body(amplitudes, ladder_ints, live_count):
    any_space = pl.BlockSpec(memory_space=pl.ANY)
    amplitudes, ladder_ints, live_count = [pltpu.with_memory_space_constraint(v, pltpu.HBM) for v in (amplitudes, ladder_ints, live_count)]
    bf16 = jnp.bfloat16
    out = pl.pallas_call(
        kernel,
        out_shape=jax.ShapeDtypeStruct((NZ * NX, 2, 256), bf16),
        in_specs=[pl.BlockSpec(memory_space=pltpu.HBM)] * 3,
        out_specs=any_space,
        scratch_shapes=[
            pltpu.VMEM((2, 128, 256), bf16),
            pltpu.VMEM((1, 256, 1024), bf16),
            pltpu.SMEM((128,), jnp.int32),
            pltpu.VMEM((NZ * NX, 2, 256), bf16),
            pltpu.VMEM((NZ * NX, 2, 256), bf16),
            pltpu.VMEM((len(GROUPS), NR, NX * 4, 256), bf16),
            pltpu.VMEM((len(GROUPS), NR - 1, NX * 4, 256), bf16),
            pltpu.VMEM((NZ * NX, 2, 256), bf16),
            pltpu.SemaphoreType.DMA((3,)),
            pltpu.SemaphoreType.DMA((NZ,)),
            pltpu.SemaphoreType.DMA((len(GROUPS),)),
            pltpu.SemaphoreType.DMA,
            pltpu.SemaphoreType.DMA,
            pltpu.SemaphoreType.DMA((len(GROUPS),)),
            pltpu.SemaphoreType.DMA,
        ],
        compiler_params=pltpu.CompilerParams(collective_id=0, has_side_effects=True, vmem_limit_bytes=8 << 20),
    )(amplitudes, ladder_ints, live_count)
    return jnp.transpose(out, (1, 0, 2))


def solution(mesh):
    in_specs = (P("pair", None, "red"), P("pair", "red", None), P())
    out_specs = P("pair", None, "red")
    return jax.shard_map(body, mesh=mesh, in_specs=in_specs, out_specs=out_specs, check_vma=False)
```

```python
import jax
import jax.numpy as jnp
from jax import lax
from jax.experimental import pallas as pl
from jax.experimental.pallas import tpu as pltpu
from jax.sharding import PartitionSpec as P

MESH = pl.DeviceIdType.MESH
NZ = 16
NX = 8
NR = 4
LAG = 4
SENDS = [8, 7, 9, 6, 10, 5, 11, 4, 12, 3, 13, 2, 14, 1, 15, 0]
GROUPS = [(0,), (1,), (2,), (3,), (4, 5), (6, 7), (15, 14), (13, 12), (8, 9), (10, 11)]


def kernel(amp_ref, w_ref, live_ref, out_ref, amp, w, live, xs, pre, rb, pb, rr, ob,
           plane, column, ready, psem, psend, lsem, bsem, rsem, osem, bsend, rsend, osend):
    me = lax.axis_index("pair")
    r = lax.axis_index("red")
    z = me // NX
    xc = lax.rem(me, NX)

    core = lax.rem(xc, 2)
    chip = xc - core
    twin = me + 1 - 2 * core

    loads = [pltpu.make_async_copy(amp_ref, amp, lsem.at[0]),
             pltpu.make_async_copy(w_ref, w, lsem.at[1]),
             pltpu.make_async_copy(live_ref, live, lsem.at[2])]
    for copy in loads:
        copy.start()

    barrier = pltpu.get_barrier_semaphore()
    for k in range(1, NX // 2):
        pl.semaphore_signal(barrier, inc=1, device_id=(z * NX + lax.rem(chip + 2 * k, NX), r), device_id_type=MESH)
    for k in range(1, NR):
        pl.semaphore_signal(barrier, inc=1, device_id=(z * NX + chip, lax.rem(r + k, NR)), device_id_type=MESH)
    for i in range(NZ - 1):
        zz = i + jnp.where(i >= z, 1, 0)
        pl.semaphore_signal(barrier, inc=1, device_id=(zz * NX + chip + 1, r), device_id_type=MESH)

    @pl.when(core == 1)
    def _():
        pl.semaphore_signal(barrier, inc=1, device_id=(twin, r), device_id_type=MESH)

    loads[0].wait()
    xs[...] = jnp.stack([amp[0], amp[1]], axis=1).reshape(NZ, NX, 2, 256)

    @pl.when(core == 0)
    def _():
        pl.semaphore_wait(barrier, NX - 1 + 2 * (NR - 1))
        pl.semaphore_signal(plane, inc=1, device_id=(twin, r), device_id_type=MESH)

    @pl.when(core == 1)
    def _():
        pl.semaphore_wait(plane, 1)

    for k in range(1, NX):
        q = lax.rem(xc + k, NX)
        pltpu.make_async_remote_copy(xs.at[:, q], pre.at[:, xc], psend, psem,
                                     device_id=(z * NX + q, r), device_id_type=MESH).start()
    pltpu.make_async_copy(xs.at[:, xc], pre.at[:, xc], psem).start()

    @pl.when(core == 1)
    def _():
        pl.semaphore_wait(barrier, 2 * (NZ - 1))
        pl.semaphore_signal(column, inc=1, device_id=(twin, r), device_id_type=MESH)
        for k in range(1, NX):
            if k % 2 == 0:
                for j in (k, k - 1):
                    pl.semaphore_signal(ready, inc=1, device_id=(z * NX + lax.rem(xc + j, NX), r), device_id_type=MESH)

    pltpu.make_async_copy(pre, pre, psem).wait()

    @pl.when(core == 0)
    def _():
        pl.semaphore_wait(column, 1)

    for dz in SENDS:
        zz = lax.rem(z + dz, NZ)
        span = pl.ds(z * NX, NX)
        if dz:
            pltpu.make_async_remote_copy(pre.at[zz], rb.at[span], bsend, bsem.at[z],
                                         device_id=(zz * NX + xc, r), device_id_type=MESH).start()
        else:
            pltpu.make_async_copy(pre.at[zz], rb.at[span], bsem.at[z]).start()

    loads[1].wait()
    loads[2].wait()
    limit = live[me] - r * 256
    rows = lax.broadcasted_iota(jnp.int32, (256, 1024), 0)
    w[0] = jnp.where(rows < limit, w[0], jnp.zeros_like(w[0]))

    def multiply(g):
        parts = []
        for zz in GROUPS[g]:
            span = pl.ds(zz * NX, NX)
            pltpu.make_async_copy(rb.at[span], rb.at[span], bsem.at[zz]).wait()
            parts.append(rb[span].reshape(NX * 2, 256))
        rows = jnp.concatenate(parts, axis=0) if len(parts) > 1 else parts[0]
        height = pl.ds(0, rows.shape[0])
        part = jnp.dot(rows, w[0], preferred_element_type=jnp.float32).astype(jnp.bfloat16)
        for j in range(NR):
            pb[g, j, height] = part[:, j * 256:(j + 1) * 256]
        for k in (2, 1, 3):
            rk = lax.rem(r + k, NR)
            pltpu.make_async_remote_copy(pb.at[g, rk, height], rr.at[g, k - 1, height], rsend.at[g], rsem.at[g],
                                         device_id=(me, rk), device_id_type=MESH).start()

    def reduce(g):
        height = pl.ds(0, len(GROUPS[g]) * NX * 2)
        landed = rr.at[g, :, height]
        pltpu.make_async_copy(landed, landed, rsem.at[g]).wait()
        total = pb[g, r, height].astype(jnp.float32)
        for k in range(NR - 1):
            total = total + rr[g, k, height].astype(jnp.float32)
        total = total.astype(jnp.bfloat16)
        for i, zz in enumerate(GROUPS[g]):
            ob[pl.ds(zz * NX, NX)] = total[i * NX * 2:(i + 1) * NX * 2].reshape(NX, 2, 256)
        for zz in GROUPS[g]:
            @pl.when(zz == z)
            def _():
                pltpu.make_async_copy(ob.at[me], out_ref.at[me], osem).start()

            @pl.when(zz != z)
            def _():
                pltpu.make_async_remote_copy(ob.at[zz * NX + xc], out_ref.at[me], osend, osem,
                                             device_id=(zz * NX + xc, r), device_id_type=MESH).start()

            for k in range(1, NX):
                p = zz * NX + lax.rem(xc + k, NX)
                pltpu.make_async_remote_copy(ob.at[p], out_ref.at[me], osend, osem,
                                             device_id=(p, r), device_id_type=MESH).start()

    for t in range(len(GROUPS) + LAG):
        if t < len(GROUPS):
            multiply(t)
        if t == LAG:
            pl.semaphore_wait(ready, NX // 2 - 1)
        if t >= LAG:
            reduce(t - LAG)

    pltpu.make_async_copy(out_ref, out_ref, osem).wait()
    pltpu.make_async_copy(xs.at[:, pl.ds(0, NX - 1)], xs.at[:, pl.ds(0, NX - 1)], psend).wait()
    pltpu.make_async_copy(pre.at[pl.ds(0, NZ - 1)], pre.at[pl.ds(0, NZ - 1)], bsend).wait()
    for g in range(len(GROUPS)):
        sent = rr.at[g, :, pl.ds(0, len(GROUPS[g]) * NX * 2)]
        pltpu.make_async_copy(sent, sent, rsend.at[g]).wait()
    pltpu.make_async_copy(ob.at[pl.ds(0, NZ * NX - 1)], ob.at[pl.ds(0, NZ * NX - 1)], osend).wait()


def body(amplitudes, ladder_ints, live_count):
    any_space = pl.BlockSpec(memory_space=pl.ANY)
    amplitudes, ladder_ints, live_count = [pltpu.with_memory_space_constraint(v, pltpu.HBM) for v in (amplitudes, ladder_ints, live_count)]
    bf16 = jnp.bfloat16
    out = pl.pallas_call(
        kernel,
        out_shape=jax.ShapeDtypeStruct((NZ * NX, 2, 256), bf16),
        in_specs=[pl.BlockSpec(memory_space=pltpu.HBM)] * 3,
        out_specs=any_space,
        scratch_shapes=[
            pltpu.VMEM((2, 128, 256), bf16),
            pltpu.VMEM((1, 256, 1024), bf16),
            pltpu.SMEM((128,), jnp.int32),
            pltpu.VMEM((NZ, NX, 2, 256), bf16),
            pltpu.VMEM((NZ, NX, 2, 256), bf16),
            pltpu.VMEM((NZ * NX, 2, 256), bf16),
            pltpu.VMEM((len(GROUPS), NR, NX * 4, 256), bf16),
            pltpu.VMEM((len(GROUPS), NR - 1, NX * 4, 256), bf16),
            pltpu.VMEM((NZ * NX, 2, 256), bf16),
            pltpu.SemaphoreType.REGULAR,
            pltpu.SemaphoreType.REGULAR,
            pltpu.SemaphoreType.REGULAR,
            pltpu.SemaphoreType.DMA,
            pltpu.SemaphoreType.DMA,
            pltpu.SemaphoreType.DMA((3,)),
            pltpu.SemaphoreType.DMA((NZ,)),
            pltpu.SemaphoreType.DMA((len(GROUPS),)),
            pltpu.SemaphoreType.DMA,
            pltpu.SemaphoreType.DMA,
            pltpu.SemaphoreType.DMA((len(GROUPS),)),
            pltpu.SemaphoreType.DMA,
        ],
        compiler_params=pltpu.CompilerParams(collective_id=0, has_side_effects=True, vmem_limit_bytes=8 << 20),
    )(amplitudes, ladder_ints, live_count)
    return jnp.transpose(out, (1, 0, 2))


def solution(mesh):
    in_specs = (P("pair", None, "red"), P("pair", "red", None), P())
    out_specs = P("pair", None, "red")
    return jax.shard_map(body, mesh=mesh, in_specs=in_specs, out_specs=out_specs, check_vma=False)
```

```python
import jax
import jax.numpy as jnp
from jax import lax
from jax.experimental import pallas as pl
from jax.experimental.pallas import tpu as pltpu
from jax.sharding import PartitionSpec as P

MESH = pl.DeviceIdType.MESH
NZ = 16
NX = 8
NR = 4
LAG = 5
SENDS = [8, 7, 9, 6, 10, 5, 11, 4, 12, 3, 13, 2, 14, 1, 15, 0]
GROUPS = [(0,), (1,), (2,), (3,), (4, 5), (6, 7), (15, 14), (13, 12), (8, 9), (10, 11)]


def kernel(amp_ref, w_ref, live_ref, out_ref, amp, w, live, xs, pre, rb, pb, rr, ob,
           plane, column, ready, psem, psend, lsem, bsem, rsem, osem, bsend, rsend, osend):
    me = lax.axis_index("pair")
    r = lax.axis_index("red")
    z = me // NX
    xc = lax.rem(me, NX)

    core = lax.rem(xc, 2)
    chip = xc - core
    twin = me + 1 - 2 * core

    barrier = pltpu.get_barrier_semaphore()

    def greet(count, first):
        for i in range(first, first + count):
            zz = i + jnp.where(i >= z, 1, 0)
            pl.semaphore_signal(barrier, inc=1, device_id=(zz * NX + chip + 1, r), device_id_type=MESH)

    greet(4, 0)
    loads = [pltpu.make_async_copy(amp_ref, amp, lsem.at[0]),
             pltpu.make_async_copy(w_ref, w, lsem.at[1]),
             pltpu.make_async_copy(live_ref, live, lsem.at[2])]
    loads[0].start()
    for k in range(1, NX // 2):
        pl.semaphore_signal(barrier, inc=1, device_id=(z * NX + lax.rem(chip + 2 * k, NX), r), device_id_type=MESH)
    for k in range(1, NR):
        pl.semaphore_signal(barrier, inc=1, device_id=(z * NX + chip, lax.rem(r + k, NR)), device_id_type=MESH)

    @pl.when(core == 1)
    def _():
        pl.semaphore_signal(barrier, inc=1, device_id=(twin, r), device_id_type=MESH)

    greet(NZ - 5, 4)
    loads[1].start()
    loads[2].start()
    loads[0].wait()
    xs[...] = jnp.stack([amp[0], amp[1]], axis=1).reshape(NZ, NX, 2, 256)

    @pl.when(core == 0)
    def _():
        pl.semaphore_wait(barrier, NX - 1 + 2 * (NR - 1))
        pl.semaphore_signal(plane, inc=1, device_id=(twin, r), device_id_type=MESH)

    @pl.when(core == 1)
    def _():
        pl.semaphore_wait(plane, 1)

    for k in range(1, NX):
        q = lax.rem(xc + k, NX)
        pltpu.make_async_remote_copy(xs.at[:, q], pre.at[:, xc], psend, psem,
                                     device_id=(z * NX + q, r), device_id_type=MESH).start()
    pltpu.make_async_copy(xs.at[:, xc], pre.at[:, xc], psem).start()

    loads[1].wait()
    loads[2].wait()
    limit = live[me] - r * 256
    rows = lax.broadcasted_iota(jnp.int32, (256, 1024), 0)
    w[0] = jnp.where(rows < limit, w[0], jnp.zeros_like(w[0]))

    @pl.when(core == 1)
    def _():
        pl.semaphore_wait(barrier, 2 * (NZ - 1))
        pl.semaphore_signal(column, inc=1, device_id=(twin, r), device_id_type=MESH)
        for k in range(1, NX):
            if k % 2 == 0:
                for j in (k, k - 1):
                    pl.semaphore_signal(ready, inc=1, device_id=(z * NX + lax.rem(xc + j, NX), r), device_id_type=MESH)

    pltpu.make_async_copy(pre, pre, psem).wait()

    @pl.when(core == 0)
    def _():
        pl.semaphore_wait(column, 1)

    for dz in SENDS:
        zz = lax.rem(z + dz, NZ)
        span = pl.ds(z * NX, NX)
        if dz:
            pltpu.make_async_remote_copy(pre.at[zz], rb.at[span], bsend, bsem.at[z],
                                         device_id=(zz * NX + xc, r), device_id_type=MESH).start()
        else:
            pltpu.make_async_copy(pre.at[zz], rb.at[span], bsem.at[z]).start()

    def multiply(g):
        parts = []
        for zz in GROUPS[g]:
            span = pl.ds(zz * NX, NX)
            pltpu.make_async_copy(rb.at[span], rb.at[span], bsem.at[zz]).wait()
            parts.append(rb[span].reshape(NX * 2, 256))
        rows = jnp.concatenate(parts, axis=0) if len(parts) > 1 else parts[0]
        height = pl.ds(0, rows.shape[0])
        part = jnp.dot(rows, w[0], preferred_element_type=jnp.float32).astype(jnp.bfloat16)
        for j in range(NR):
            pb[g, j, height] = part[:, j * 256:(j + 1) * 256]
        for i in range(NR - 1):
            rk = i + jnp.where(i >= r, 1, 0)
            slot = r - jnp.where(i >= r, 0, 1)
            pltpu.make_async_remote_copy(pb.at[g, rk, height], rr.at[g, slot, height], rsend.at[g], rsem.at[g],
                                         device_id=(me, rk), device_id_type=MESH).start()

    def reduce(g):
        height = pl.ds(0, len(GROUPS[g]) * NX * 2)
        landed = rr.at[g, :, height]
        pltpu.make_async_copy(landed, landed, rsem.at[g]).wait()
        total = pb[g, r, height].astype(jnp.float32)
        for k in range(NR - 1):
            total = total + rr[g, k, height].astype(jnp.float32)
        total = total.astype(jnp.bfloat16)
        for i, zz in enumerate(GROUPS[g]):
            ob[pl.ds(zz * NX, NX)] = total[i * NX * 2:(i + 1) * NX * 2].reshape(NX, 2, 256)
        for zz in GROUPS[g]:
            if zz == 0:
                for p in (1, 0, 2, 3, 6, 7, 4, 5):
                    @pl.when(p != me)
                    def _():
                        pltpu.make_async_remote_copy(ob.at[p], out_ref.at[me], osend, osem,
                                                     device_id=(p, r), device_id_type=MESH).start()

                    @pl.when(p == me)
                    def _():
                        pltpu.make_async_copy(ob.at[p], out_ref.at[me], osem).start()

                continue

            @pl.when(zz == z)
            def _():
                pltpu.make_async_copy(ob.at[me], out_ref.at[me], osem).start()

            @pl.when(zz != z)
            def _():
                pltpu.make_async_remote_copy(ob.at[zz * NX + xc], out_ref.at[me], osend, osem,
                                             device_id=(zz * NX + xc, r), device_id_type=MESH).start()

            for k in range(1, NX):
                p = zz * NX + lax.rem(xc + k, NX)
                pltpu.make_async_remote_copy(ob.at[p], out_ref.at[me], osend, osem,
                                             device_id=(p, r), device_id_type=MESH).start()

    for t in range(len(GROUPS) + LAG):
        if t < len(GROUPS):
            multiply(t)
        if t == LAG:
            pl.semaphore_wait(ready, NX // 2 - 1)
        if t >= LAG:
            reduce(t - LAG)

    pltpu.make_async_copy(out_ref, out_ref, osem).wait()
    pltpu.make_async_copy(xs.at[:, pl.ds(0, NX - 1)], xs.at[:, pl.ds(0, NX - 1)], psend).wait()
    pltpu.make_async_copy(pre.at[pl.ds(0, NZ - 1)], pre.at[pl.ds(0, NZ - 1)], bsend).wait()
    for g in range(len(GROUPS)):
        sent = rr.at[g, :, pl.ds(0, len(GROUPS[g]) * NX * 2)]
        pltpu.make_async_copy(sent, sent, rsend.at[g]).wait()
    pltpu.make_async_copy(ob.at[pl.ds(0, NZ * NX - 1)], ob.at[pl.ds(0, NZ * NX - 1)], osend).wait()


def body(amplitudes, ladder_ints, live_count):
    any_space = pl.BlockSpec(memory_space=pl.ANY)
    amplitudes, ladder_ints, live_count = [pltpu.with_memory_space_constraint(v, pltpu.HBM) for v in (amplitudes, ladder_ints, live_count)]
    bf16 = jnp.bfloat16
    out = pl.pallas_call(
        kernel,
        out_shape=jax.ShapeDtypeStruct((NZ * NX, 2, 256), bf16),
        in_specs=[pl.BlockSpec(memory_space=pltpu.HBM)] * 3,
        out_specs=any_space,
        scratch_shapes=[
            pltpu.VMEM((2, 128, 256), bf16),
            pltpu.VMEM((1, 256, 1024), bf16),
            pltpu.SMEM((128,), jnp.int32),
            pltpu.VMEM((NZ, NX, 2, 256), bf16),
            pltpu.VMEM((NZ, NX, 2, 256), bf16),
            pltpu.VMEM((NZ * NX, 2, 256), bf16),
            pltpu.VMEM((len(GROUPS), NR, NX * 4, 256), bf16),
            pltpu.VMEM((len(GROUPS), NR - 1, NX * 4, 256), bf16),
            pltpu.VMEM((NZ * NX, 2, 256), bf16),
            pltpu.SemaphoreType.REGULAR,
            pltpu.SemaphoreType.REGULAR,
            pltpu.SemaphoreType.REGULAR,
            pltpu.SemaphoreType.DMA,
            pltpu.SemaphoreType.DMA,
            pltpu.SemaphoreType.DMA((3,)),
            pltpu.SemaphoreType.DMA((NZ,)),
            pltpu.SemaphoreType.DMA((len(GROUPS),)),
            pltpu.SemaphoreType.DMA,
            pltpu.SemaphoreType.DMA,
            pltpu.SemaphoreType.DMA((len(GROUPS),)),
            pltpu.SemaphoreType.DMA,
        ],
        compiler_params=pltpu.CompilerParams(collective_id=0, has_side_effects=True, vmem_limit_bytes=8 << 20),
    )(amplitudes, ladder_ints, live_count)
    return jnp.transpose(out, (1, 0, 2))


def solution(mesh):
    in_specs = (P("pair", None, "red"), P("pair", "red", None), P())
    out_specs = P("pair", None, "red")
    return jax.shard_map(body, mesh=mesh, in_specs=in_specs, out_specs=out_specs, check_vma=False)
```

```python
import jax
import jax.numpy as jnp
from jax import lax
from jax.experimental import pallas as pl
from jax.experimental.pallas import tpu as pltpu
from jax.sharding import PartitionSpec as P

MESH = pl.DeviceIdType.MESH
NZ = 16
NX = 8
NR = 4
LAG = 5
SENDS = [8, 7, 9, 6, 10, 5, 11, 4, 12, 3, 13, 2, 14, 1, 15, 0]
OTHER = [1, 15, 2, 14, 3, 13, 4, 12, 5, 11, 6, 10, 7, 9, 8, 0]
GROUPS = [(0,), (1,), (2,), (3,), (4, 5), (6, 7), (15, 14), (13, 12), (8, 9), (10, 11)]


def kernel(amp_ref, w_ref, live_ref, out_ref, amp, w, live, xs, pre, rb, pb, rr, ob,
           plane, column, ready, psem, psend, lsem, bsem, rsem, osem, bsend, rsend, osend):
    me = lax.axis_index("pair")
    r = lax.axis_index("red")
    z = me // NX
    xc = lax.rem(me, NX)

    core = lax.rem(xc, 2)
    chip = xc - core
    twin = me + 1 - 2 * core

    barrier = pltpu.get_barrier_semaphore()

    def greet(count, first):
        for i in range(first, first + count):
            zz = i + jnp.where(i >= z, 1, 0)
            pl.semaphore_signal(barrier, inc=1, device_id=(zz * NX + chip + 1, r), device_id_type=MESH)

    greet(4, 0)
    loads = [pltpu.make_async_copy(amp_ref, amp, lsem.at[0]),
             pltpu.make_async_copy(w_ref, w, lsem.at[1]),
             pltpu.make_async_copy(live_ref, live, lsem.at[2])]
    loads[0].start()
    for k in range(1, NX // 2):
        pl.semaphore_signal(barrier, inc=1, device_id=(z * NX + lax.rem(chip + 2 * k, NX), r), device_id_type=MESH)
    for k in range(1, NR):
        pl.semaphore_signal(barrier, inc=1, device_id=(z * NX + chip, lax.rem(r + k, NR)), device_id_type=MESH)

    @pl.when(core == 1)
    def _():
        pl.semaphore_signal(barrier, inc=1, device_id=(twin, r), device_id_type=MESH)

    greet(NZ - 5, 4)
    loads[1].start()
    loads[2].start()
    loads[0].wait()
    xs[...] = jnp.stack([amp[0], amp[1]], axis=1).reshape(NZ, NX, 2, 256)

    @pl.when(core == 0)
    def _():
        pl.semaphore_wait(barrier, NX - 1 + 2 * (NR - 1))
        pl.semaphore_signal(plane, inc=1, device_id=(twin, r), device_id_type=MESH)

    @pl.when(core == 1)
    def _():
        pl.semaphore_wait(plane, 1)

    for k in range(1, NX):
        q = lax.rem(xc + k, NX)
        pltpu.make_async_remote_copy(xs.at[:, q], pre.at[:, xc], psend, psem,
                                     device_id=(z * NX + q, r), device_id_type=MESH).start()
    pltpu.make_async_copy(xs.at[:, xc], pre.at[:, xc], psem).start()

    loads[1].wait()
    loads[2].wait()
    limit = live[me] - r * 256
    rows = lax.broadcasted_iota(jnp.int32, (256, 1024), 0)
    w[0] = jnp.where(rows < limit, w[0], jnp.zeros_like(w[0]))

    @pl.when(core == 1)
    def _():
        pl.semaphore_wait(barrier, 2 * (NZ - 1))
        pl.semaphore_signal(column, inc=1, device_id=(twin, r), device_id_type=MESH)
        for k in range(1, NX):
            if k % 2 == 0:
                for j in (k, k - 1):
                    pl.semaphore_signal(ready, inc=1, device_id=(z * NX + lax.rem(xc + j, NX), r), device_id_type=MESH)

    pltpu.make_async_copy(pre, pre, psem).wait()

    @pl.when(core == 0)
    def _():
        pl.semaphore_wait(column, 1)

    late = z >= NZ // 2
    span = pl.ds(z * NX, NX)
    for dz, other in zip(SENDS, OTHER):
        zz = lax.rem(z + jnp.where(late, jnp.where(core == 0, NZ - other, other), jnp.where(core == 0, NZ - dz, dz)), NZ)
        if dz:
            pltpu.make_async_remote_copy(pre.at[zz], rb.at[span], bsend, bsem.at[z],
                                         device_id=(zz * NX + xc, r), device_id_type=MESH).start()
        else:
            pltpu.make_async_copy(pre.at[z], rb.at[span], bsem.at[z]).start()

    def multiply(g):
        parts = []
        for zz in GROUPS[g]:
            span = pl.ds(zz * NX, NX)
            pltpu.make_async_copy(rb.at[span], rb.at[span], bsem.at[zz]).wait()
            parts.append(rb[span].reshape(NX * 2, 256))
        rows = jnp.concatenate(parts, axis=0) if len(parts) > 1 else parts[0]
        height = pl.ds(0, rows.shape[0])
        part = jnp.dot(rows, w[0], preferred_element_type=jnp.float32).astype(jnp.bfloat16)
        for j in range(NR):
            pb[g, j, height] = part[:, j * 256:(j + 1) * 256]
        for i in range(NR - 1):
            rk = i + jnp.where(i >= r, 1, 0)
            slot = r - jnp.where(i >= r, 0, 1)
            pltpu.make_async_remote_copy(pb.at[g, rk, height], rr.at[g, slot, height], rsend.at[g], rsem.at[g],
                                         device_id=(me, rk), device_id_type=MESH).start()

    def reduce(g):
        height = pl.ds(0, len(GROUPS[g]) * NX * 2)
        landed = rr.at[g, :, height]
        pltpu.make_async_copy(landed, landed, rsem.at[g]).wait()
        total = pb[g, r, height].astype(jnp.float32)
        for k in range(NR - 1):
            total = total + rr[g, k, height].astype(jnp.float32)
        total = total.astype(jnp.bfloat16)
        for i, zz in enumerate(GROUPS[g]):
            ob[pl.ds(zz * NX, NX)] = total[i * NX * 2:(i + 1) * NX * 2].reshape(NX, 2, 256)
        for zz in GROUPS[g]:
            if zz == 0:
                for p in (1, 0, 2, 3, 6, 7, 4, 5):
                    @pl.when(p != me)
                    def _():
                        pltpu.make_async_remote_copy(ob.at[p], out_ref.at[me], osend, osem,
                                                     device_id=(p, r), device_id_type=MESH).start()

                    @pl.when(p == me)
                    def _():
                        pltpu.make_async_copy(ob.at[p], out_ref.at[me], osem).start()

                continue

            @pl.when(zz == z)
            def _():
                pltpu.make_async_copy(ob.at[me], out_ref.at[me], osem).start()

            @pl.when(zz != z)
            def _():
                pltpu.make_async_remote_copy(ob.at[zz * NX + xc], out_ref.at[me], osend, osem,
                                             device_id=(zz * NX + xc, r), device_id_type=MESH).start()

            for k in range(1, NX):
                p = zz * NX + lax.rem(xc + k, NX)
                pltpu.make_async_remote_copy(ob.at[p], out_ref.at[me], osend, osem,
                                             device_id=(p, r), device_id_type=MESH).start()

    for t in range(len(GROUPS) + LAG):
        if t < len(GROUPS):
            multiply(t)
        if t == LAG:
            pl.semaphore_wait(ready, NX // 2 - 1)
        if t >= LAG:
            reduce(t - LAG)

    pltpu.make_async_copy(out_ref, out_ref, osem).wait()
    pltpu.make_async_copy(xs.at[:, pl.ds(0, NX - 1)], xs.at[:, pl.ds(0, NX - 1)], psend).wait()
    pltpu.make_async_copy(pre.at[pl.ds(0, NZ - 1)], pre.at[pl.ds(0, NZ - 1)], bsend).wait()
    for g in range(len(GROUPS)):
        sent = rr.at[g, :, pl.ds(0, len(GROUPS[g]) * NX * 2)]
        pltpu.make_async_copy(sent, sent, rsend.at[g]).wait()
    pltpu.make_async_copy(ob.at[pl.ds(0, NZ * NX - 1)], ob.at[pl.ds(0, NZ * NX - 1)], osend).wait()


def body(amplitudes, ladder_ints, live_count):
    any_space = pl.BlockSpec(memory_space=pl.ANY)
    amplitudes, ladder_ints, live_count = [pltpu.with_memory_space_constraint(v, pltpu.HBM) for v in (amplitudes, ladder_ints, live_count)]
    bf16 = jnp.bfloat16
    out = pl.pallas_call(
        kernel,
        out_shape=jax.ShapeDtypeStruct((NZ * NX, 2, 256), bf16),
        in_specs=[pl.BlockSpec(memory_space=pltpu.HBM)] * 3,
        out_specs=any_space,
        scratch_shapes=[
            pltpu.VMEM((2, 128, 256), bf16),
            pltpu.VMEM((1, 256, 1024), bf16),
            pltpu.SMEM((128,), jnp.int32),
            pltpu.VMEM((NZ, NX, 2, 256), bf16),
            pltpu.VMEM((NZ, NX, 2, 256), bf16),
            pltpu.VMEM((NZ * NX, 2, 256), bf16),
            pltpu.VMEM((len(GROUPS), NR, NX * 4, 256), bf16),
            pltpu.VMEM((len(GROUPS), NR - 1, NX * 4, 256), bf16),
            pltpu.VMEM((NZ * NX, 2, 256), bf16),
            pltpu.SemaphoreType.REGULAR,
            pltpu.SemaphoreType.REGULAR,
            pltpu.SemaphoreType.REGULAR,
            pltpu.SemaphoreType.DMA,
            pltpu.SemaphoreType.DMA,
            pltpu.SemaphoreType.DMA((3,)),
            pltpu.SemaphoreType.DMA((NZ,)),
            pltpu.SemaphoreType.DMA((len(GROUPS),)),
            pltpu.SemaphoreType.DMA,
            pltpu.SemaphoreType.DMA,
            pltpu.SemaphoreType.DMA((len(GROUPS),)),
            pltpu.SemaphoreType.DMA,
        ],
        compiler_params=pltpu.CompilerParams(collective_id=0, has_side_effects=True, vmem_limit_bytes=8 << 20),
    )(amplitudes, ladder_ints, live_count)
    return jnp.transpose(out, (1, 0, 2))


def solution(mesh):
    in_specs = (P("pair", None, "red"), P("pair", "red", None), P())
    out_specs = P("pair", None, "red")
    return jax.shard_map(body, mesh=mesh, in_specs=in_specs, out_specs=out_specs, check_vma=False)
```

```python
import jax
import jax.numpy as jnp
from jax import lax
from jax.experimental import pallas as pl
from jax.experimental.pallas import tpu as pltpu
from jax.sharding import PartitionSpec as P

MESH = pl.DeviceIdType.MESH
NZ = 16
NX = 8
NR = 4
LAG = 5
SENDS = [8, 7, 9, 6, 10, 5, 11, 4, 12, 3, 13, 2, 14, 1, 15, 0]
OTHER = [1, 15, 2, 14, 3, 13, 4, 12, 5, 11, 6, 10, 7, 9, 8, 0]
GROUPS = [(0,), (1,), (2,), (3,), (4, 5), (6, 7), (15, 14), (13, 12), (8, 9), (10, 11)]


def kernel(amp_ref, w_ref, live_ref, out_ref, amp, w, live, xs, pre, rb, pb, rr, ob,
           plane, column, ready, psem, psend, lsem, bsem, rsem, osem, bsend, rsend, osend):
    me = lax.axis_index("pair")
    r = lax.axis_index("red")
    z = me // NX
    xc = lax.rem(me, NX)

    core = lax.rem(xc, 2)
    chip = xc - core
    twin = me + 1 - 2 * core

    barrier = pltpu.get_barrier_semaphore()

    def greet(count, first):
        for i in range(first, first + count):
            zz = i + jnp.where(i >= z, 1, 0)
            pl.semaphore_signal(barrier, inc=1, device_id=(zz * NX + chip + 1, r), device_id_type=MESH)

    greet(4, 0)
    loads = [pltpu.make_async_copy(amp_ref, amp, lsem.at[0]),
             pltpu.make_async_copy(w_ref, w, lsem.at[1]),
             pltpu.make_async_copy(live_ref, live, lsem.at[2])]
    loads[0].start()
    for k in range(1, NX // 2):
        pl.semaphore_signal(barrier, inc=1, device_id=(z * NX + lax.rem(chip + 2 * k, NX), r), device_id_type=MESH)
    for k in range(1, NR):
        pl.semaphore_signal(barrier, inc=1, device_id=(z * NX + chip, lax.rem(r + k, NR)), device_id_type=MESH)

    @pl.when(core == 1)
    def _():
        pl.semaphore_signal(barrier, inc=1, device_id=(twin, r), device_id_type=MESH)

    greet(NZ - 5, 4)
    loads[1].start()
    loads[2].start()
    loads[0].wait()
    xs[...] = jnp.stack([amp[0], amp[1]], axis=1).reshape(NZ, NX, 2, 256)

    @pl.when(core == 0)
    def _():
        pl.semaphore_wait(barrier, NX - 1 + 2 * (NR - 1))
        pl.semaphore_signal(plane, inc=1, device_id=(twin, r), device_id_type=MESH)

    @pl.when(core == 1)
    def _():
        pl.semaphore_wait(plane, 1)

    for k in range(1, NX):
        q = lax.rem(xc + k, NX)
        pltpu.make_async_remote_copy(xs.at[:, q], pre.at[:, xc], psend, psem,
                                     device_id=(z * NX + q, r), device_id_type=MESH).start()
    pltpu.make_async_copy(xs.at[:, xc], pre.at[:, xc], psem).start()

    loads[1].wait()
    loads[2].wait()
    limit = live[me] - r * 256
    rows = lax.broadcasted_iota(jnp.int32, (256, 1024), 0)
    w[0] = jnp.where(rows < limit, w[0], jnp.zeros_like(w[0]))

    @pl.when(core == 1)
    def _():
        pl.semaphore_wait(barrier, 2 * (NZ - 1))
        pl.semaphore_signal(column, inc=1, device_id=(twin, r), device_id_type=MESH)
        for k in range(1, NX):
            if k % 2 == 0:
                for j in (k, k - 1):
                    pl.semaphore_signal(ready, inc=1, device_id=(z * NX + lax.rem(xc + j, NX), r), device_id_type=MESH)

    pltpu.make_async_copy(pre, pre, psem).wait()

    @pl.when(core == 0)
    def _():
        pl.semaphore_wait(column, 1)

    late = z >= NZ // 2
    span = pl.ds(z * NX, NX)
    for dz, other in zip(SENDS, OTHER):
        zz = lax.rem(z + jnp.where(late, jnp.where(core == 0, NZ - other, other), jnp.where(core == 0, NZ - dz, dz)), NZ)
        if dz:
            pltpu.make_async_remote_copy(pre.at[zz], rb.at[span], bsend, bsem.at[z],
                                         device_id=(zz * NX + xc, r), device_id_type=MESH).start()
        else:
            pltpu.make_async_copy(pre.at[z], rb.at[span], bsem.at[z]).start()

    def multiply(g):
        parts = []
        for zz in GROUPS[g]:
            span = pl.ds(zz * NX, NX)
            pltpu.make_async_copy(rb.at[span], rb.at[span], bsem.at[zz]).wait()
            parts.append(rb[span].reshape(NX * 2, 256))
        rows = jnp.concatenate(parts, axis=0) if len(parts) > 1 else parts[0]
        height = pl.ds(0, rows.shape[0])
        part = jnp.dot(rows, w[0], preferred_element_type=jnp.float32).astype(jnp.bfloat16)
        for j in range(NR):
            pb[g, j, height] = part[:, j * 256:(j + 1) * 256]
        for i in range(NR - 1):
            rk = i + jnp.where(i >= r, 1, 0)
            slot = r - jnp.where(i >= r, 0, 1)
            pltpu.make_async_remote_copy(pb.at[g, rk, height], rr.at[g, slot, height], rsend.at[g], rsem.at[g],
                                         device_id=(me, rk), device_id_type=MESH).start()

    def reduce(g):
        height = pl.ds(0, len(GROUPS[g]) * NX * 2)
        landed = rr.at[g, :, height]
        pltpu.make_async_copy(landed, landed, rsem.at[g]).wait()
        total = pb[g, r, height].astype(jnp.float32)
        for k in range(NR - 1):
            total = total + rr[g, k, height].astype(jnp.float32)
        total = total.astype(jnp.bfloat16)
        for i, zz in enumerate(GROUPS[g]):
            ob[pl.ds(zz * NX, NX)] = total[i * NX * 2:(i + 1) * NX * 2].reshape(NX, 2, 256)
        for zz in GROUPS[g]:
            if zz == 0:
                for p in (1, 0, 2, 3, 6, 7, 4, 5):
                    @pl.when(p != me)
                    def _():
                        pltpu.make_async_remote_copy(ob.at[p], out_ref.at[me], osend, osem,
                                                     device_id=(p, r), device_id_type=MESH).start()

                    @pl.when(p == me)
                    def _():
                        pltpu.make_async_copy(ob.at[p], out_ref.at[me], osem).start()

                continue

            @pl.when(zz == z)
            def _():
                pltpu.make_async_copy(ob.at[me], out_ref.at[me], osem).start()

            @pl.when(zz != z)
            def _():
                pltpu.make_async_remote_copy(ob.at[zz * NX + xc], out_ref.at[me], osend, osem,
                                             device_id=(zz * NX + xc, r), device_id_type=MESH).start()

            for k in range(1, NX):
                p = zz * NX + lax.rem(xc + k, NX)
                pltpu.make_async_remote_copy(ob.at[p], out_ref.at[me], osend, osem,
                                             device_id=(p, r), device_id_type=MESH).start()

    for t in range(len(GROUPS) + LAG):
        if t < len(GROUPS):
            multiply(t)
        if t == LAG:
            pl.semaphore_wait(ready, NX // 2 - 1)
        if t >= LAG:
            reduce(t - LAG)

    pltpu.make_async_copy(xs.at[:, pl.ds(0, NX - 1)], xs.at[:, pl.ds(0, NX - 1)], psend).wait()
    pltpu.make_async_copy(pre.at[pl.ds(0, NZ - 1)], pre.at[pl.ds(0, NZ - 1)], bsend).wait()
    for g in range(len(GROUPS)):
        sent = rr.at[g, :, pl.ds(0, len(GROUPS[g]) * NX * 2)]
        pltpu.make_async_copy(sent, sent, rsend.at[g]).wait()
    pltpu.make_async_copy(ob.at[pl.ds(0, NZ * NX - 1)], ob.at[pl.ds(0, NZ * NX - 1)], osend).wait()
    pltpu.make_async_copy(out_ref, out_ref, osem).wait()


def body(amplitudes, ladder_ints, live_count):
    any_space = pl.BlockSpec(memory_space=pl.ANY)
    amplitudes, ladder_ints, live_count = [pltpu.with_memory_space_constraint(v, pltpu.HBM) for v in (amplitudes, ladder_ints, live_count)]
    bf16 = jnp.bfloat16
    out = pl.pallas_call(
        kernel,
        out_shape=jax.ShapeDtypeStruct((NZ * NX, 2, 256), bf16),
        in_specs=[pl.BlockSpec(memory_space=pltpu.HBM)] * 3,
        out_specs=any_space,
        scratch_shapes=[
            pltpu.VMEM((2, 128, 256), bf16),
            pltpu.VMEM((1, 256, 1024), bf16),
            pltpu.SMEM((128,), jnp.int32),
            pltpu.VMEM((NZ, NX, 2, 256), bf16),
            pltpu.VMEM((NZ, NX, 2, 256), bf16),
            pltpu.VMEM((NZ * NX, 2, 256), bf16),
            pltpu.VMEM((len(GROUPS), NR, NX * 4, 256), bf16),
            pltpu.VMEM((len(GROUPS), NR - 1, NX * 4, 256), bf16),
            pltpu.VMEM((NZ * NX, 2, 256), bf16),
            pltpu.SemaphoreType.REGULAR,
            pltpu.SemaphoreType.REGULAR,
            pltpu.SemaphoreType.REGULAR,
            pltpu.SemaphoreType.DMA,
            pltpu.SemaphoreType.DMA,
            pltpu.SemaphoreType.DMA((3,)),
            pltpu.SemaphoreType.DMA((NZ,)),
            pltpu.SemaphoreType.DMA((len(GROUPS),)),
            pltpu.SemaphoreType.DMA,
            pltpu.SemaphoreType.DMA,
            pltpu.SemaphoreType.DMA((len(GROUPS),)),
            pltpu.SemaphoreType.DMA,
        ],
        compiler_params=pltpu.CompilerParams(collective_id=0, has_side_effects=True, vmem_limit_bytes=8 << 20),
    )(amplitudes, ladder_ints, live_count)
    return jnp.transpose(out, (1, 0, 2))


def solution(mesh):
    in_specs = (P("pair", None, "red"), P("pair", "red", None), P())
    out_specs = P("pair", None, "red")
    return jax.shard_map(body, mesh=mesh, in_specs=in_specs, out_specs=out_specs, check_vma=False)
```

```python
import jax
import jax.numpy as jnp
from jax import lax
from jax.experimental import pallas as pl
from jax.experimental.pallas import tpu as pltpu
from jax.sharding import PartitionSpec as P

MESH = pl.DeviceIdType.MESH
NZ = 16
NX = 8
NR = 4
LAG = 5
SENDS = [8, 7, 9, 6, 10, 5, 11, 4, 12, 3, 13, 2, 14, 1, 15, 0]
OTHER = [1, 15, 2, 14, 3, 13, 4, 12, 5, 11, 6, 10, 7, 9, 8, 0]
GROUPS = [(0,), (1,), (2,), (3,), (4, 5), (6, 7), (15, 14), (13, 12), (8, 9), (10, 11)]


def kernel(amp_ref, w_ref, live_ref, out_ref, amp, w, live, xs, pre, rb, pb, rr, ob,
           plane, column, ready, psem, psend, lsem, bsem, rsem, osem, bsend, rsend, osend):
    me = lax.axis_index("pair")
    r = lax.axis_index("red")
    z = me // NX
    xc = lax.rem(me, NX)

    core = lax.rem(xc, 2)
    chip = xc - core
    twin = me + 1 - 2 * core

    barrier = pltpu.get_barrier_semaphore()

    def greet(count, first):
        for i in range(first, first + count):
            zz = i + jnp.where(i >= z, 1, 0)
            pl.semaphore_signal(barrier, inc=1, device_id=(zz * NX + chip + 1, r), device_id_type=MESH)

    greet(4, 0)
    loads = [pltpu.make_async_copy(amp_ref, amp, lsem.at[0]),
             pltpu.make_async_copy(w_ref, w, lsem.at[1]),
             pltpu.make_async_copy(live_ref, live, lsem.at[2])]
    loads[0].start()
    for k in range(1, NX // 2):
        pl.semaphore_signal(barrier, inc=1, device_id=(z * NX + lax.rem(chip + 2 * k, NX), r), device_id_type=MESH)
    for k in range(1, NR):
        pl.semaphore_signal(barrier, inc=1, device_id=(z * NX + chip, lax.rem(r + k, NR)), device_id_type=MESH)

    @pl.when(core == 1)
    def _():
        pl.semaphore_signal(barrier, inc=1, device_id=(twin, r), device_id_type=MESH)

    greet(NZ - 5, 4)
    loads[1].start()
    loads[2].start()
    loads[0].wait()
    xs[...] = jnp.stack([amp[0], amp[1]], axis=1).reshape(NZ, NX, 2, 256)

    @pl.when(core == 0)
    def _():
        pl.semaphore_wait(barrier, NX - 1 + 2 * (NR - 1))
        pl.semaphore_signal(plane, inc=1, device_id=(twin, r), device_id_type=MESH)

    @pl.when(core == 1)
    def _():
        pl.semaphore_wait(plane, 1)

    for k in range(1, NX):
        q = lax.rem(xc + k, NX)
        pltpu.make_async_remote_copy(xs.at[:, q], pre.at[:, xc], psend, psem,
                                     device_id=(z * NX + q, r), device_id_type=MESH).start()
    pltpu.make_async_copy(xs.at[:, xc], pre.at[:, xc], psem).start()

    loads[1].wait()
    loads[2].wait()
    limit = live[me] - r * 256
    rows = lax.broadcasted_iota(jnp.int32, (256, 1024), 0)
    w[0] = jnp.where(rows < limit, w[0], jnp.zeros_like(w[0]))

    @pl.when(core == 1)
    def _():
        pl.semaphore_wait(barrier, 2 * (NZ - 1))
        pl.semaphore_signal(column, inc=1, device_id=(twin, r), device_id_type=MESH)

    pltpu.make_async_copy(pre, pre, psem).wait()

    @pl.when(core == 0)
    def _():
        pl.semaphore_wait(column, 1)

    late = z >= NZ // 2
    span = pl.ds(z * NX, NX)
    for dz, other in zip(SENDS, OTHER):
        zz = lax.rem(z + jnp.where(late, jnp.where(core == 0, NZ - other, other), jnp.where(core == 0, NZ - dz, dz)), NZ)
        if dz:
            pltpu.make_async_remote_copy(pre.at[zz], rb.at[span], bsend, bsem.at[z],
                                         device_id=(zz * NX + xc, r), device_id_type=MESH).start()
        else:
            pltpu.make_async_copy(pre.at[z], rb.at[span], bsem.at[z]).start()

    @pl.when(core == 1)
    def _():
        for k in range(1, NX):
            if k % 2 == 0:
                for j in (k, k - 1):
                    pl.semaphore_signal(ready, inc=1, device_id=(z * NX + lax.rem(xc + j, NX), r), device_id_type=MESH)

    def multiply(g):
        parts = []
        for zz in GROUPS[g]:
            span = pl.ds(zz * NX, NX)
            pltpu.make_async_copy(rb.at[span], rb.at[span], bsem.at[zz]).wait()
            parts.append(rb[span].reshape(NX * 2, 256))
        rows = jnp.concatenate(parts, axis=0) if len(parts) > 1 else parts[0]
        height = pl.ds(0, rows.shape[0])
        part = jnp.dot(rows, w[0], preferred_element_type=jnp.float32).astype(jnp.bfloat16)
        for j in range(NR):
            pb[g, j, height] = part[:, j * 256:(j + 1) * 256]
        for i in range(NR - 1):
            rk = i + jnp.where(i >= r, 1, 0)
            slot = r - jnp.where(i >= r, 0, 1)
            pltpu.make_async_remote_copy(pb.at[g, rk, height], rr.at[g, slot, height], rsend.at[g], rsem.at[g],
                                         device_id=(me, rk), device_id_type=MESH).start()

    def reduce(g):
        height = pl.ds(0, len(GROUPS[g]) * NX * 2)
        landed = rr.at[g, :, height]
        pltpu.make_async_copy(landed, landed, rsem.at[g]).wait()
        total = pb[g, r, height].astype(jnp.float32)
        for k in range(NR - 1):
            total = total + rr[g, k, height].astype(jnp.float32)
        total = total.astype(jnp.bfloat16)
        for i, zz in enumerate(GROUPS[g]):
            ob[pl.ds(zz * NX, NX)] = total[i * NX * 2:(i + 1) * NX * 2].reshape(NX, 2, 256)
        for zz in GROUPS[g]:
            if zz == 0:
                for p in (1, 0, 2, 3, 6, 7, 4, 5):
                    @pl.when(p != me)
                    def _():
                        pltpu.make_async_remote_copy(ob.at[p], out_ref.at[me], osend, osem,
                                                     device_id=(p, r), device_id_type=MESH).start()

                    @pl.when(p == me)
                    def _():
                        pltpu.make_async_copy(ob.at[p], out_ref.at[me], osem).start()

                continue

            @pl.when(zz == z)
            def _():
                pltpu.make_async_copy(ob.at[me], out_ref.at[me], osem).start()

            @pl.when(zz != z)
            def _():
                pltpu.make_async_remote_copy(ob.at[zz * NX + xc], out_ref.at[me], osend, osem,
                                             device_id=(zz * NX + xc, r), device_id_type=MESH).start()

            for k in range(1, NX):
                p = zz * NX + lax.rem(xc + k, NX)
                pltpu.make_async_remote_copy(ob.at[p], out_ref.at[me], osend, osem,
                                             device_id=(p, r), device_id_type=MESH).start()

    for t in range(len(GROUPS) + LAG):
        if t < len(GROUPS):
            multiply(t)
        if t == LAG:
            pl.semaphore_wait(ready, NX // 2 - 1)
        if t >= LAG:
            reduce(t - LAG)

    pltpu.make_async_copy(xs.at[:, pl.ds(0, NX - 1)], xs.at[:, pl.ds(0, NX - 1)], psend).wait()
    pltpu.make_async_copy(pre.at[pl.ds(0, NZ - 1)], pre.at[pl.ds(0, NZ - 1)], bsend).wait()
    for g in range(len(GROUPS)):
        sent = rr.at[g, :, pl.ds(0, len(GROUPS[g]) * NX * 2)]
        pltpu.make_async_copy(sent, sent, rsend.at[g]).wait()
    pltpu.make_async_copy(ob.at[pl.ds(0, NZ * NX - 1)], ob.at[pl.ds(0, NZ * NX - 1)], osend).wait()
    pltpu.make_async_copy(out_ref, out_ref, osem).wait()


def body(amplitudes, ladder_ints, live_count):
    any_space = pl.BlockSpec(memory_space=pl.ANY)
    amplitudes, ladder_ints, live_count = [pltpu.with_memory_space_constraint(v, pltpu.HBM) for v in (amplitudes, ladder_ints, live_count)]
    bf16 = jnp.bfloat16
    out = pl.pallas_call(
        kernel,
        out_shape=jax.ShapeDtypeStruct((NZ * NX, 2, 256), bf16),
        in_specs=[pl.BlockSpec(memory_space=pltpu.HBM)] * 3,
        out_specs=any_space,
        scratch_shapes=[
            pltpu.VMEM((2, 128, 256), bf16),
            pltpu.VMEM((1, 256, 1024), bf16),
            pltpu.SMEM((128,), jnp.int32),
            pltpu.VMEM((NZ, NX, 2, 256), bf16),
            pltpu.VMEM((NZ, NX, 2, 256), bf16),
            pltpu.VMEM((NZ * NX, 2, 256), bf16),
            pltpu.VMEM((len(GROUPS), NR, NX * 4, 256), bf16),
            pltpu.VMEM((len(GROUPS), NR - 1, NX * 4, 256), bf16),
            pltpu.VMEM((NZ * NX, 2, 256), bf16),
            pltpu.SemaphoreType.REGULAR,
            pltpu.SemaphoreType.REGULAR,
            pltpu.SemaphoreType.REGULAR,
            pltpu.SemaphoreType.DMA,
            pltpu.SemaphoreType.DMA,
            pltpu.SemaphoreType.DMA((3,)),
            pltpu.SemaphoreType.DMA((NZ,)),
            pltpu.SemaphoreType.DMA((len(GROUPS),)),
            pltpu.SemaphoreType.DMA,
            pltpu.SemaphoreType.DMA,
            pltpu.SemaphoreType.DMA((len(GROUPS),)),
            pltpu.SemaphoreType.DMA,
        ],
        compiler_params=pltpu.CompilerParams(collective_id=0, has_side_effects=True, vmem_limit_bytes=8 << 20),
    )(amplitudes, ladder_ints, live_count)
    return jnp.transpose(out, (1, 0, 2))


def solution(mesh):
    in_specs = (P("pair", None, "red"), P("pair", "red", None), P())
    out_specs = P("pair", None, "red")
    return jax.shard_map(body, mesh=mesh, in_specs=in_specs, out_specs=out_specs, check_vma=False)
```
